32 devices in a mesh: dp: 32 (over z, y, x, core).
Axes of the slice: x: 2, y: 2, z: 4, core: 2. Of those that a mesh axis runs over, the one named last changes fastest.
Arguments:
- hidden_in: bfloat16 [4096, 640], P('dp'), may hold values from -6 to 6
- segment_ids: int32 [4096], P('dp'), may hold values from 0 to 3, never falling along the last dimension, each value on 1 to 2048 neighbouring positions
- cotangent: bfloat16 [4096, 640], P('dp'), may hold values from -6 to 6
- query_weight: bfloat16 [640, 1024], P(None, 'dp'), may hold values from -0.25 to 0.25
- key_weight: bfloat16 [640, 256], P(None, 'dp'), may hold values from -0.25 to 0.25
- value_weight: bfloat16 [640, 256], P(None, 'dp'), may hold values from -0.25 to 0.25
- out_weight: bfloat16 [1024, 640], P('dp'), may hold values from -0.1875 to 0.1875
- gate_weight: bfloat16 [640, 2048], P(None, 'dp'), may hold values from -0.25 to 0.25
- up_weight: bfloat16 [640, 2048], P(None, 'dp'), may hold values from -0.25 to 0.25
- down_weight: bfloat16 [2048, 640], P('dp'), may hold values from -0.125 to 0.125
- gain_attn: float32 [640], replicated, may hold values from 0.1 to 1.9
- gain_query: float32 [256], replicated, may hold values from 0.1 to 1.9
- gain_key: float32 [256], replicated, may hold values from 0.1 to 1.9
- gain_post: float32 [640], replicated, may hold values from 0.1 to 1.9
- gain_ffw: float32 [640], replicated, may hold values from 0.1 to 1.9
- gain_final: float32 [640], replicated, may hold values from 0.1 to 1.9
Outputs:
- output: bfloat16 [4096, 640], P('dp')
- input_grad: bfloat16 [4096, 640], P('dp')
- query_grad: float32 [640, 1024], P(None, 'dp')
- key_grad: float32 [640, 256], P(None, 'dp')
- value_grad: float32 [640, 256], P(None, 'dp')
- out_grad: float32 [1024, 640], P('dp')
- gate_grad: float32 [640, 2048], P(None, 'dp')
- up_grad: float32 [640, 2048], P(None, 'dp')
- down_grad: float32 [2048, 640], P('dp')
- grad_gattn: float32 [640], replicated
- grad_gquery: float32 [256], replicated
- grad_gkey: float32 [256], replicated
- grad_gpost: float32 [640], replicated
- grad_gffw: float32 [640], replicated
- grad_gfinal: float32 [640], replicated
The draws below stay inside these ranges and needn't reach their ends.
Inputs may be any that keep to these rules, and one draw needn't show every extreme that they name: `segment_ids`: ids never fall along the tokens; every id appears; each sequence holds 1 to 2048 tokens, one exactly 2048.
All inputs are finite; a program needn't handle non-finite values.
Results may differ from the reference program's by a relative error of at most 0.017.
Values may be sent and summed in bfloat16 or wider, within the bound.
No kernel may reach another device: no remote copies, remote signals or barrier semaphores. Data moves between devices by JAX's collectives and lax.ppermute only.
A program may use at most 128 MiB of HBM per device.

```python
import math
import jax
import jax.numpy as jnp
import numpy as np
from jax import lax

D = 640
H = 4
HD = 256
FF = 2048
WINDOW = 512
MAXLEN = 2048
TOKENS = 4096
SEQS = 4


def level_of(rng, shape, shards, low, top_value):
    loudness, own = 1.0, jax.random.fold_in(rng, 6)
    for dim, parts in shards:
        heights = jnp.exp(jax.random.uniform(jax.random.fold_in(own, dim), (parts,), jnp.float32, low / len(shards), top_value / len(shards)))
        loudness = loudness * jnp.repeat(heights, shape[dim] // parts).reshape([-1 if axis == dim else 1 for axis in range(len(shape))])
    return loudness


def length_profile(number_of, total, reach, slope):
    loads = [(1 << 20) // math.isqrt(grade ** slope) + 1 for grade in range(2, number_of + 1)]
    surplus, given = total - reach - (number_of - 1), [1] * (number_of - 1)
    while surplus > 0:
        movable = [i for i in range(number_of - 1) if given[i] < reach]
        pool, left = sum([loads[i] for i in movable]), surplus
        for i in movable:
            addition = min(reach - given[i], max(1, left * loads[i] // pool), surplus)
            given[i] = given[i] + addition
            surplus = surplus - addition
    return np.array([reach] + given)


def ragged(rng, count, total, most, lean):
    if count == 2:
        one = jax.random.randint(rng, (), max(1, total - most), min(most, total - 1) + 1)
        return jnp.stack([one, total - one])
    tallies = jnp.asarray(length_profile(count, total, most, lean), jnp.int32)
    couples = (count - 1) // 2
    donor, receiver = tallies[1:1 + 2 * couples:2], tallies[2:2 + 2 * couples:2]
    slack = jnp.minimum(donor - 1, most - receiver)
    moved = jax.random.randint(jax.random.fold_in(rng, 1), (couples,), 0, 1 << 20) % (slack + 1)
    tallies = tallies.at[1:1 + 2 * couples:2].set(donor - moved).at[2:2 + 2 * couples:2].set(receiver + moved)
    return tallies[jax.random.permutation(jax.random.fold_in(rng, 2), count)]


def centred(stream_key, shape, width, most, split=(), kind=jnp.bfloat16):
    result = jax.random.normal(stream_key, shape, jnp.float32) * width
    if len(split) > 0:
        result = level_of(stream_key, shape, split, -0.22, 0.18) * result
    return jnp.clip(result, min=-most, max=most).astype(kind)


def setup_inputs(seed: int = 0) -> dict:
    seeds = jax.random.split(jax.random.key(seed), 17)
    hidden_in = centred(seeds[0], (TOKENS, D), 1.0, 6.0, ((0, 32),))
    segment_ids = jnp.searchsorted(jnp.cumsum(ragged(seeds[1], SEQS, TOKENS, MAXLEN, 2)), jnp.arange(TOKENS), side="right").astype(jnp.int32)
    cotangent = centred(seeds[2], (TOKENS, D), 1.0, 6.0, ((0, 32),))
    query_weight = centred(seeds[3], (D, H * HD), D ** -0.5, 0.25, ((1, 32),))
    key_weight = centred(seeds[4], (D, HD), D ** -0.5, 0.25, ((1, 32),))
    value_weight = centred(seeds[5], (D, HD), D ** -0.5, 0.25, ((1, 32),))
    out_weight = centred(seeds[6], (H * HD, D), (H * HD) ** -0.5, 0.1875, ((0, 32),))
    gate_weight = centred(seeds[7], (D, FF), D ** -0.5, 0.25, ((1, 32),))
    up_weight = centred(seeds[8], (D, FF), D ** -0.5, 0.25, ((1, 32),))
    down_weight = centred(seeds[9], (FF, D), FF ** -0.5, 0.125, ((0, 32),))
    gain_attn = jnp.clip(1.0 + 0.18 * jax.random.normal(seeds[10], (D,), jnp.float32), 0.1, 1.9)
    gain_query = jnp.clip(1.0 + 0.18 * jax.random.normal(seeds[11], (HD,), jnp.float32), 0.1, 1.9)
    gain_key = jnp.clip(1.0 + 0.18 * jax.random.normal(seeds[12], (HD,), jnp.float32), 0.1, 1.9)
    gain_post = jnp.clip(1.0 + 0.18 * jax.random.normal(seeds[13], (D,), jnp.float32), 0.1, 1.9)
    gain_ffw = jnp.clip(1.0 + 0.18 * jax.random.normal(seeds[14], (D,), jnp.float32), 0.1, 1.9)
    gain_final = jnp.clip(1.0 + 0.18 * jax.random.normal(seeds[15], (D,), jnp.float32), 0.1, 1.9)
    return {"hidden_in": hidden_in, "segment_ids": segment_ids, "cotangent": cotangent, "query_weight": query_weight, "key_weight": key_weight, "value_weight": value_weight, "out_weight": out_weight, "gate_weight": gate_weight, "up_weight": up_weight, "down_weight": down_weight, "gain_attn": gain_attn, "gain_query": gain_query, "gain_key": gain_key, "gain_post": gain_post, "gain_ffw": gain_ffw, "gain_final": gain_final}


EPS = 1e-06
SCALE = 0.0625
BASE = 10000.0

def rms_scale(value, gain):
    mean_sq = lax.optimization_barrier(jnp.mean(value * value, axis=-1, keepdims=True))
    return value * lax.rsqrt(mean_sq + EPS) * gain

def rotate(value, cosine, sine):
    half = value.shape[-1] // 2
    first = value[..., :half]
    second = value[..., half:]
    return jnp.concatenate([first * cosine - second * sine, second * cosine + first * sine], axis=-1)

def angles(positions):
    freq = jnp.power(BASE, -(jnp.arange(HD // 2, dtype=jnp.float32) * (2.0 / HD)))
    theta = positions.astype(jnp.float32)[:, None] * freq[None, :]
    return (jnp.cos(theta), jnp.sin(theta))

def prep_query(flat, gain, cosine, sine):
    heads = flat.reshape(flat.shape[0], H, HD)
    return rotate(rms_scale(heads, gain), cosine[:, None, :], sine[:, None, :]) * SCALE

def prep_key(flat, gain, cosine, sine):
    return rotate(rms_scale(flat, gain), cosine, sine)

def gelu_tanh(value):
    return jax.nn.gelu(value, approximate=True)

def norm_back(value, gain, incoming):
    _, pull = jax.vjp(rms_scale, value, gain)
    return pull(incoming)

def reference(hidden_in, segment_ids, cotangent, query_weight, key_weight, value_weight, out_weight, gate_weight, up_weight, down_weight, gain_attn, gain_query, gain_key, gain_post, gain_ffw, gain_final):
    total = hidden_in.shape[0]
    block = min(512, total)
    count = total // block
    f32 = jnp.float32
    bf16 = jnp.bfloat16
    index = jnp.arange(total, dtype=jnp.int32)
    previous = jnp.concatenate([jnp.full((1,), -1, jnp.int32), segment_ids[:-1]])
    starts = lax.cummax(jnp.where(segment_ids != previous, index, 0), axis=0)
    positions = index - starts
    cosine, sine = angles(positions)

    def key_block(item):
        rows_x, cos_b, sin_b = item
        normed = rms_scale(rows_x.astype(f32), gain_attn).astype(bf16)
        key = jnp.dot(normed, key_weight, preferred_element_type=f32)
        value = jnp.dot(normed, value_weight, preferred_element_type=f32)
        return (prep_key(key, gain_key, cos_b, sin_b).astype(bf16), value.astype(bf16))
    key_all, value_all = lax.map(key_block, (hidden_in.reshape(count, block, D), cosine.reshape(count, block, HD // 2), sine.reshape(count, block, HD // 2)))
    pad = jnp.zeros((WINDOW, HD), bf16)
    key_pad = jnp.concatenate([pad, key_all.reshape(total, HD)], axis=0)
    value_pad = jnp.concatenate([pad, value_all.reshape(total, HD)], axis=0)
    span = block + WINDOW

    def step(carry, which):
        q_acc, o_acc, g_acc, u_acc, d_acc, gq_acc, gp_acc, gf_acc, gz_acc, dkeys, dvalues = carry
        start = (which * block).astype(jnp.int32)
        xf = lax.dynamic_slice_in_dim(hidden_in, start, block, 0).astype(f32)
        cot = lax.dynamic_slice_in_dim(cotangent, start, block, 0).astype(f32)
        st = lax.dynamic_slice_in_dim(starts, start, block, 0)
        cos_b = lax.dynamic_slice_in_dim(cosine, start, block, 0)
        sin_b = lax.dynamic_slice_in_dim(sine, start, block, 0)
        keys = lax.dynamic_slice_in_dim(key_pad, start, span, 0)
        values = lax.dynamic_slice_in_dim(value_pad, start, span, 0)
        gi = start + jnp.arange(block, dtype=jnp.int32)
        gj = start - WINDOW + jnp.arange(span, dtype=jnp.int32)
        mask = (gj[None, :] >= st[:, None]) & (gj[None, :] <= gi[:, None]) & (gi[:, None] - gj[None, :] < WINDOW)
        normed = rms_scale(xf, gain_attn).astype(bf16)
        query = jnp.dot(normed, query_weight, preferred_element_type=f32)
        qrot = prep_query(query, gain_query, cos_b, sin_b).astype(bf16)
        scores = jnp.einsum('lhd,md->lhm', qrot.astype(f32), keys.astype(f32))
        wide = mask[:, None, :]
        lse = jnp.log(lax.optimization_barrier(jnp.sum(jnp.where(wide, jnp.exp(scores), 0.0), axis=-1, keepdims=True)))
        prob = jnp.where(wide, jnp.exp(scores - lse), 0.0)
        prob_b = prob.astype(bf16)
        mixed3 = jnp.einsum('lhm,md->lhd', prob_b.astype(f32), values.astype(f32)).astype(bf16)
        mixed = mixed3.reshape(block, H * HD)
        attn = jnp.dot(mixed, out_weight, preferred_element_type=f32)
        resid = xf + rms_scale(attn, gain_post)
        ffw_in = rms_scale(resid, gain_ffw).astype(bf16)
        gate = jnp.dot(ffw_in, gate_weight, preferred_element_type=f32)
        up = jnp.dot(ffw_in, up_weight, preferred_element_type=f32)
        hidden = (gelu_tanh(gate) * up).astype(bf16)
        ffw_out = jnp.dot(hidden, down_weight, preferred_element_type=f32)
        out_rows = (resid + rms_scale(ffw_out, gain_final)).astype(bf16)
        d_ffw, g_final = norm_back(ffw_out, gain_final, cot)
        d_ffw_b = d_ffw.astype(bf16)
        d_acc = d_acc + jnp.dot(hidden.T, d_ffw_b, preferred_element_type=f32)
        d_hidden = jnp.dot(d_ffw_b, down_weight.T, preferred_element_type=f32)
        gel, gpull = jax.vjp(gelu_tanh, gate)
        d_gate = gpull(d_hidden * up)[0].astype(bf16)
        d_up = (d_hidden * gel).astype(bf16)
        g_acc = g_acc + jnp.dot(ffw_in.T, d_gate, preferred_element_type=f32)
        u_acc = u_acc + jnp.dot(ffw_in.T, d_up, preferred_element_type=f32)
        d_ffwin = jnp.dot(d_gate, gate_weight.T, preferred_element_type=f32) + jnp.dot(d_up, up_weight.T, preferred_element_type=f32)
        d_res_n, g_ffw = norm_back(resid, gain_ffw, d_ffwin)
        d_resid = cot + d_res_n
        d_attn, g_post = norm_back(attn, gain_post, d_resid)
        d_attn_b = d_attn.astype(bf16)
        o_acc = o_acc + jnp.dot(mixed.T, d_attn_b, preferred_element_type=f32)
        d_mixed = jnp.dot(d_attn_b, out_weight.T, preferred_element_type=f32).astype(bf16).reshape(block, H, HD)
        d_probs = jnp.einsum('lhd,md->lhm', d_mixed.astype(f32), values.astype(f32))
        delta = lax.optimization_barrier(jnp.sum(d_mixed.astype(f32) * mixed3.astype(f32), axis=-1, keepdims=True))
        d_scores = (prob * (d_probs - delta)).astype(bf16)
        d_qrot = jnp.einsum('lhm,md->lhd', d_scores.astype(f32), keys.astype(f32))
        d_keys = jnp.einsum('lhm,lhd->md', d_scores.astype(f32), qrot.astype(f32))
        d_vals = jnp.einsum('lhm,lhd->md', prob_b.astype(f32), d_mixed.astype(f32))
        dkeys = lax.dynamic_update_slice_in_dim(dkeys, lax.dynamic_slice_in_dim(dkeys, start, span, 0) + d_keys, start, 0)
        dvalues = lax.dynamic_update_slice_in_dim(dvalues, lax.dynamic_slice_in_dim(dvalues, start, span, 0) + d_vals, start, 0)
        _, qpull = jax.vjp(lambda a, g: prep_query(a, g, cos_b, sin_b), query, gain_query)
        d_query, g_query = qpull(d_qrot)
        d_query_b = d_query.astype(bf16)
        q_acc = q_acc + jnp.dot(normed.T, d_query_b, preferred_element_type=f32)
        d_part = jnp.dot(d_query_b, query_weight.T, preferred_element_type=f32)
        carry = (q_acc, o_acc, g_acc, u_acc, d_acc, gq_acc + g_query, gp_acc + g_post, gf_acc + g_ffw, gz_acc + g_final, dkeys, dvalues)
        return (carry, (out_rows, d_resid, d_part))
    init = (jnp.zeros((D, H * HD), f32), jnp.zeros((H * HD, D), f32), jnp.zeros((D, FF), f32), jnp.zeros((D, FF), f32), jnp.zeros((FF, D), f32), jnp.zeros((HD,), f32), jnp.zeros((D,), f32), jnp.zeros((D,), f32), jnp.zeros((D,), f32), jnp.zeros((total + WINDOW, HD), f32), jnp.zeros((total + WINDOW, HD), f32))
    carry, (out_all, d_resid_all, d_part_all) = lax.scan(step, init, jnp.arange(count, dtype=jnp.int32))
    q_acc, o_acc, g_acc, u_acc, d_acc, gq_acc, gp_acc, gf_acc, gz_acc, dkeys, dvalues = carry
    d_resid_all = d_resid_all.reshape(total, D)
    d_part_all = d_part_all.reshape(total, D)

    def finish(carry, which):
        k_acc, v_acc, gk_acc, ga_acc = carry
        start = (which * block).astype(jnp.int32)
        xf = lax.dynamic_slice_in_dim(hidden_in, start, block, 0).astype(f32)
        cos_b = lax.dynamic_slice_in_dim(cosine, start, block, 0)
        sin_b = lax.dynamic_slice_in_dim(sine, start, block, 0)
        d_krot = lax.dynamic_slice_in_dim(dkeys, start + WINDOW, block, 0)
        d_vb = lax.dynamic_slice_in_dim(dvalues, start + WINDOW, block, 0)
        normed = rms_scale(xf, gain_attn).astype(bf16)
        key = jnp.dot(normed, key_weight, preferred_element_type=f32)
        _, kpull = jax.vjp(lambda a, g: prep_key(a, g, cos_b, sin_b), key, gain_key)
        d_key, g_key = kpull(d_krot)
        d_key_b = d_key.astype(bf16)
        d_val_b = d_vb.astype(bf16)
        k_acc = k_acc + jnp.dot(normed.T, d_key_b, preferred_element_type=f32)
        v_acc = v_acc + jnp.dot(normed.T, d_val_b, preferred_element_type=f32)
        d_normed = lax.dynamic_slice_in_dim(d_part_all, start, block, 0) + jnp.dot(d_key_b, key_weight.T, preferred_element_type=f32) + jnp.dot(d_val_b, value_weight.T, preferred_element_type=f32)
        d_in, g_attn = norm_back(xf, gain_attn, d_normed)
        grad_rows = (lax.dynamic_slice_in_dim(d_resid_all, start, block, 0) + d_in).astype(bf16)
        return ((k_acc, v_acc, gk_acc + g_key, ga_acc + g_attn), grad_rows)
    init2 = (jnp.zeros((D, HD), f32), jnp.zeros((D, HD), f32), jnp.zeros((HD,), f32), jnp.zeros((D,), f32))
    (k_acc, v_acc, gk_acc, ga_acc), grad_all = lax.scan(finish, init2, jnp.arange(count, dtype=jnp.int32))
    output = out_all.reshape(total, D)
    input_grad = grad_all.reshape(total, D)
    return (output, input_grad, q_acc, k_acc, v_acc, o_acc, g_acc, u_acc, d_acc, ga_acc, gq_acc, gk_acc, gp_acc, gf_acc, gz_acc)
```

```python
import jax
import jax.numpy as jnp
from jax import lax
from jax.sharding import PartitionSpec as P

H = 4
HD = 256
WINDOW = 512

EPS = 1e-06
SCALE = 0.0625
BASE = 10000.0


f32 = jnp.float32
bf16 = jnp.bfloat16


def swap(array, mask):
    peers = lax.axis_size("dp")
    return lax.ppermute(array, "dp", [(i, i ^ mask) for i in range(peers)])


def shifted(array, by):
    peers = lax.axis_size("dp")
    pairs = [(i, i + by) for i in range(peers) if 0 <= i + by < peers]
    return lax.ppermute(array, "dp", pairs)


def plan(peers):
    quad = peers // 4
    middle = []
    mask = 2
    while mask < quad:
        middle.append(mask)
        mask = mask * 2
    return middle, quad


def gather(shard, order, quad):
    got = jnp.stack([shard] + [swap(shard, k * quad) for k in (1, 2, 3)])
    for mask in order[:-1]:
        got = jnp.stack([got, swap(got, mask)])
    other = swap(got, order[-1])
    return jnp.stack(
        [jnp.stack([got, other]), jnp.stack([swap(got, 1), swap(other, 1)])]
    )


def scatter(parts, order, quad):
    for mask in [1] + order[::-1]:
        parts = (parts[0].astype(f32) + swap(parts[1], mask).astype(f32)).astype(bf16)
    total = parts[0].astype(f32)
    for k in (1, 2, 3):
        total = total + swap(parts[k], k * quad).astype(f32)
    return total


def total_sum(array, peers):
    mask = 1
    while mask < peers:
        array = array + swap(array, mask)
        mask = mask * 2
    return array


def rms_scale(value, gain):
    mean_sq = jnp.mean(value * value, axis=-1, keepdims=True)
    return value * lax.rsqrt(mean_sq + EPS) * gain


def rotate(value, cosine, sine):
    half = value.shape[-1] // 2
    first = value[..., :half]
    second = value[..., half:]
    return jnp.concatenate(
        [first * cosine - second * sine, second * cosine + first * sine], axis=-1
    )


def prep_query(flat, gain, cosine, sine):
    heads = flat.reshape(flat.shape[0], H, HD)
    return rotate(rms_scale(heads, gain), cosine[:, None, :], sine[:, None, :]) * SCALE


def prep_key(flat, gain, cosine, sine):
    return rotate(rms_scale(flat, gain), cosine, sine)


def gelu_tanh(value):
    return jax.nn.gelu(value, approximate=True)


def norm_back(value, gain, incoming):
    _, pull = jax.vjp(rms_scale, value, gain)
    return pull(incoming)


def xor_blocks(vector, blocks, bits):
    rows = vector.reshape(blocks, -1)
    mask = 1
    while mask < blocks:
        pairs = rows.reshape(blocks // (2 * mask), 2, mask, -1)
        rows = jnp.where((bits & mask) != 0, pairs[:, ::-1], pairs).reshape(blocks, -1)
        mask = mask * 2
    return rows.reshape(vector.shape)


def dot_t(left, right):
    return lax.dot_general(
        left, right, (((left.ndim - 1,), (right.ndim - 1,)), ((), ())), preferred_element_type=f32
    )


def dot_n(left, right):
    return jnp.dot(left, right, preferred_element_type=f32)


def dot_g(left, right):
    return lax.dot_general(left, right, (((0,), (0,)), ((), ())), preferred_element_type=f32)


def body(
    hidden_in,
    segment_ids,
    cotangent,
    query_weight,
    key_weight,
    value_weight,
    out_weight,
    gate_weight,
    up_weight,
    down_weight,
    gain_attn,
    gain_query,
    gain_key,
    gain_post,
    gain_ffw,
    gain_final,
):
    peers = lax.axis_size("dp")
    me = lax.axis_index("dp")
    middle, quad = plan(peers)
    forth, back = middle, middle[::-1]
    count = len(middle)
    rows, width = hidden_in.shape
    reach = (WINDOW + rows - 1) // rows
    halo = reach * rows
    span = halo + rows
    q_block = query_weight.shape[1]
    k_block = key_weight.shape[1]
    f_block = gate_weight.shape[1]
    f_half = f_block // 2
    twos = (2,) * count

    ids = jnp.zeros((8, width), bf16).at[0, :rows].set(segment_ids.astype(bf16))
    mine = jnp.concatenate([hidden_in, ids], axis=0)
    before = [shifted(mine, hop) for hop in range(reach, 0, -1)]

    qt, kt, vt, gt, ut = (w.T for w in (query_weight, key_weight, value_weight, gate_weight, up_weight))
    qkv_all = gather(jnp.concatenate([qt, kt, vt], axis=0), forth, quad)
    o_all = gather(out_weight, back, quad)
    ff_a = gather(jnp.concatenate([gt[:f_half], ut[:f_half], down_weight[:f_half]], axis=0), forth, quad)
    ff_b = gather(jnp.concatenate([gt[f_half:], ut[f_half:], down_weight[f_half:]], axis=0), back, quad)

    tail = (count + 2, count + 3)
    to_slots = (count + 1,) + tuple(range(1, count + 1)) + (0,) + tail
    to_slots_b = (count + 1,) + tuple(range(count, 0, -1)) + (0,) + tail
    qkv_slots = qkv_all.transpose(to_slots).reshape(peers, q_block + 2 * k_block, width)
    o_slots = o_all.transpose(to_slots_b).reshape(peers * q_block, width)
    q_rows = qkv_slots[:, :q_block].reshape(peers * q_block, width)
    k_slots = qkv_slots[:, q_block : q_block + k_block].reshape(HD, width)
    v_slots = qkv_slots[:, q_block + k_block :].reshape(HD, width)

    per_head = peers // H
    bits = me & (per_head - 1)
    place = jnp.arange(HD, dtype=jnp.int32)
    feature = ((place // q_block) ^ bits) * q_block + place % q_block
    source = (me ^ (feature // k_block)) * k_block + feature % k_block
    pick = (source[:, None] == place[None, :]).astype(bf16)
    k_rows = dot_n(pick, k_slots).astype(bf16)
    v_rows = dot_n(pick, v_slots).astype(bf16)
    gq = xor_blocks(gain_query, per_head, bits)
    gk = xor_blocks(gain_key, per_head, bits)
    half = HD // 2
    freq = jnp.power(BASE, -((feature[:half] % half).astype(f32) * (2.0 / HD)))
    theta = jnp.arange(span, dtype=jnp.int32).astype(f32)[:, None] * freq[None, :]
    cosine = jnp.cos(theta)
    sine = jnp.sin(theta) * jnp.where(feature[0] >= half, -1.0, 1.0)
    cos_q, sin_q = cosine[halo:], sine[halo:]

    window = jnp.concatenate([b[:rows] for b in before] + [hidden_in], axis=0).astype(f32)
    seg = segment_ids.astype(f32)
    key_seg = jnp.concatenate([b[rows, :rows].astype(f32) for b in before] + [seg])
    base = me * rows
    gidx = base + jnp.arange(rows, dtype=jnp.int32)
    key_idx = base - halo + jnp.arange(span, dtype=jnp.int32)
    mask = (
        (key_seg[None, :] == seg[:, None])
        & (key_idx[None, :] <= gidx[:, None])
        & (gidx[:, None] - key_idx[None, :] < WINDOW)
        & (key_idx[None, :] >= 0)
    )
    wide = mask[:, None, :]

    xf = hidden_in.astype(f32)
    normed_all = rms_scale(window, gain_attn).astype(bf16)
    normed = normed_all[halo:]
    query = dot_t(normed, q_rows)
    key = dot_t(normed_all, k_rows)
    values = dot_t(normed_all, v_rows).astype(bf16)
    qrot = prep_query(query, gq, cos_q, sin_q).astype(bf16)
    keys = prep_key(key, gk, cosine, sine).astype(bf16)
    scores = jnp.einsum("lhd,md->lhm", qrot, keys, preferred_element_type=f32)
    lse = jnp.log(jnp.sum(jnp.where(wide, jnp.exp(scores), 0.0), axis=-1, keepdims=True))
    prob_b = jnp.where(wide, jnp.exp(scores - lse), 0.0).astype(bf16)
    mixed3 = jnp.einsum("lhm,md->lhd", prob_b, values, preferred_element_type=f32).astype(bf16)
    mixed = mixed3.reshape(rows, H * HD)
    attn = dot_n(mixed, o_slots)
    resid = xf + rms_scale(attn, gain_post)
    ffw_in = rms_scale(resid, gain_ffw).astype(bf16)

    def ff_split(array):
        flat = array.reshape(peers, 3 * f_half, width)
        return [flat[:, i * f_half : (i + 1) * f_half].reshape(peers * f_half, width) for i in range(3)]

    halves = []
    ffw_out = 0.0
    for array in (ff_a, ff_b):
        g_rows, u_rows, d_rows = ff_split(array)
        gate = dot_t(ffw_in, g_rows)
        up = dot_t(ffw_in, u_rows)
        gel, gpull = jax.vjp(gelu_tanh, gate)
        hidden = (gel * up).astype(bf16)
        ffw_out = ffw_out + dot_n(hidden, d_rows)
        halves.append((g_rows, u_rows, d_rows, up, gel, gpull, hidden))
    output = (resid + rms_scale(ffw_out, gain_final)).astype(bf16)

    cot = cotangent.astype(f32)
    d_ffw, g_final = norm_back(ffw_out, gain_final, cot)
    d_ffw_b = d_ffw.astype(bf16)
    d_ffwin = 0.0
    ff_sums = []
    for (g_rows, u_rows, d_rows, up, gel, gpull, hidden), order in zip(halves, (forth, back)):
        d_hidden = dot_t(d_ffw_b, d_rows)
        d_gate = gpull(d_hidden * up)[0].astype(bf16)
        d_up = (d_hidden * gel).astype(bf16)
        d_ffwin = d_ffwin + dot_n(d_gate, g_rows) + dot_n(d_up, u_rows)
        grads = [dot_g(d_gate, ffw_in), dot_g(d_up, ffw_in), dot_g(hidden, d_ffw_b)]
        grads = [g.astype(bf16).reshape(peers, f_half, width) for g in grads]
        grads = jnp.concatenate(grads, axis=1).reshape((2,) + twos + (4, 3 * f_half, width))
        ff_sums.append(scatter(grads, order, quad))
    d_res_n, g_ffw = norm_back(resid, gain_ffw, d_ffwin)
    d_resid = cot + d_res_n
    d_attn, g_post = norm_back(attn, gain_post, d_resid)
    d_attn_b = d_attn.astype(bf16)
    o_grad = dot_g(mixed, d_attn_b).astype(bf16)
    d_mixed = dot_t(d_attn_b, o_slots).astype(bf16).reshape(rows, H, HD)
    prob = jnp.where(wide, jnp.exp(scores - lse), 0.0)
    d_probs = jnp.einsum("lhd,md->lhm", d_mixed, values, preferred_element_type=f32)
    delta = jnp.sum(d_mixed.astype(f32) * mixed3.astype(f32), axis=-1, keepdims=True)
    d_scores = (prob * (d_probs - delta)).astype(bf16)
    d_qrot = jnp.einsum("lhm,md->lhd", d_scores, keys, preferred_element_type=f32)
    d_keys = jnp.einsum("lhm,lhd->md", d_scores, qrot, preferred_element_type=f32)
    d_values = jnp.einsum("lhm,lhd->md", prob_b, d_mixed, preferred_element_type=f32)
    _, qpull = jax.vjp(lambda a, g: prep_query(a, g, cos_q, sin_q), query, gq)
    d_query, g_query = qpull(d_qrot)
    _, kpull = jax.vjp(lambda a, g: prep_key(a, g, cosine, sine), key, gk)
    d_key, g_key = kpull(d_keys)
    d_query_b = d_query.astype(bf16)
    d_key_b = d_key.astype(bf16)
    d_val_b = d_values.astype(bf16)
    d_window = dot_n(d_key_b, k_rows) + dot_n(d_val_b, v_rows)
    d_normed = dot_n(d_query_b, q_rows) + d_window[halo:]
    for hop in range(1, reach + 1):
        low = (reach - hop) * rows
        d_normed = d_normed + shifted(d_window[low : low + rows].astype(bf16), -hop).astype(f32)
    d_in, g_attn = norm_back(xf, gain_attn, d_normed)
    input_grad = (d_resid + d_in).astype(bf16)

    d_key_s = dot_n(d_key_b, pick).astype(bf16)
    d_val_s = dot_n(d_val_b, pick).astype(bf16)
    q_grad = dot_g(d_query_b, normed).astype(bf16).reshape(peers, q_block, width)
    k_grad = dot_g(d_key_s, normed_all).astype(bf16).reshape(peers, k_block, width)
    v_grad = dot_g(d_val_s, normed_all).astype(bf16).reshape(peers, k_block, width)
    lead = (4,) + twos + (2,)
    from_slots = (count + 1,) + tuple(range(1, count + 1)) + (0,) + tail
    from_slots_b = (count + 1,) + tuple(range(count, 0, -1)) + (0,) + tail
    qkv_grads = jnp.concatenate([q_grad, k_grad, v_grad], axis=1)
    qkv_grads = qkv_grads.reshape(lead + qkv_grads.shape[1:]).transpose(from_slots)
    o_grads = o_grad.reshape(lead + (q_block, width)).transpose(from_slots_b)
    o_sum = scatter(o_grads, back, quad)
    qkv_sum = scatter(qkv_grads, forth, quad)

    g_query = xor_blocks(g_query, per_head, bits)
    g_key = xor_blocks(g_key, per_head, bits)
    gains = jnp.concatenate([g_attn, g_post, g_ffw, g_final, g_query, g_key])
    gains = total_sum(gains.reshape(-1, 128), peers).reshape(-1)
    sums = []
    at = 0
    for size in (width, width, width, width, HD, HD):
        sums.append(gains[at : at + size])
        at = at + size
    sum_attn, sum_post, sum_ffw, sum_final, sum_query, sum_key = sums

    def joined(i):
        return jnp.concatenate([s[i * f_half : (i + 1) * f_half] for s in ff_sums], axis=0)

    return (
        output,
        input_grad,
        qkv_sum[:q_block].T,
        qkv_sum[q_block : q_block + k_block].T,
        qkv_sum[q_block + k_block :].T,
        o_sum,
        joined(0).T,
        joined(1).T,
        joined(2),
        sum_attn,
        sum_query,
        sum_key,
        sum_post,
        sum_ffw,
        sum_final,
    )


def solution(mesh):
    rows = P("dp", None)
    columns = P(None, "dp")
    in_specs = (rows, P("dp"), rows, columns, columns, columns, rows, columns, columns, rows) + (P(),) * 6
    out_specs = (rows, rows, columns, columns, columns, rows, columns, columns, rows) + (P(),) * 6
    return jax.shard_map(body, mesh=mesh, in_specs=in_specs, out_specs=out_specs, check_vma=False)
```

```python
import jax
import jax.numpy as jnp
from jax import lax
from jax.experimental import pallas as pl
from jax.experimental.pallas import tpu as pltpu
from jax.sharding import PartitionSpec as P


H = 4
HD = 256
WINDOW = 512

EPS = 1e-06
SCALE = 0.0625
BASE = 10000.0


f32 = jnp.float32
bf16 = jnp.bfloat16


def swap(array, mask):
    peers = lax.axis_size("dp")
    return lax.ppermute(array, "dp", [(i, i ^ mask) for i in range(peers)])


def shifted(array, by):
    peers = lax.axis_size("dp")
    pairs = [(i, i + by) for i in range(peers) if 0 <= i + by < peers]
    return lax.ppermute(array, "dp", pairs)


def plan(peers):
    quad = peers // 4
    middle = []
    mask = 2
    while mask < quad:
        middle.append(mask)
        mask = mask * 2
    return middle, quad


def widen(shard, order):
    for mask in order[:-1]:
        shard = lax.optimization_barrier(jnp.stack([shard, swap(shard, mask)]))
    return shard


def finish(shard, order):
    other = swap(shard, order[-1])
    return [shard, other, swap(shard, 1), swap(other, 1)]


def quad_swaps(shard, quad):
    return [shard] + [swap(shard, k * quad) for k in (1, 2, 3)]


def plus(left, right):
    return (left.astype(f32) + right.astype(f32)).astype(bf16)


def quad_sum(parts, quad):
    got = [swap(parts[k], k * quad).astype(f32) for k in (1, 2, 3)]
    return (parts[0].astype(f32) + got[0]) + (got[1] + got[2])


def after(array, first):
    return lax.optimization_barrier((array, first))[0]


def added(*terms):
    total = terms[0].astype(f32)
    for term in terms[1:]:
        total = total + term.astype(f32)
    return total.astype(bf16)


def rms_rate(value):
    return lax.rsqrt(jnp.mean(value * value, axis=-1, keepdims=True) + EPS)


def norm_grad(value, rate, gain, incoming):
    scaled = incoming * gain
    inner = jnp.mean(scaled * value, axis=-1, keepdims=True)
    dv = rate * (scaled - value * (rate * rate * inner))
    return dv, jnp.sum(incoming * value * rate, axis=0, keepdims=True)


def turn(value, cosine, sine):
    half = value.shape[-1] // 2
    first, second = value[:, :half], value[:, half:]
    return jnp.concatenate([first * cosine - second * sine, second * cosine + first * sine], axis=-1)


def turn_back(value, cosine, sine):
    half = value.shape[-1] // 2
    first, second = value[:, :half], value[:, half:]
    return jnp.concatenate([first * cosine + second * sine, second * cosine - first * sine], axis=-1)


def xor_blocks(vector, blocks, bits):
    rows = vector.reshape(blocks, -1)
    mask = 1
    while mask < blocks:
        pairs = rows.reshape(blocks // (2 * mask), 2, mask, -1)
        rows = jnp.where((bits & mask) != 0, pairs[:, ::-1], pairs).reshape(blocks, -1)
        mask = mask * 2
    return rows.reshape(vector.shape)


def dot_t(left, right):
    return lax.dot_general(left, right, (((1,), (1,)), ((), ())), preferred_element_type=f32)


def dot_n(left, right):
    return jnp.dot(left, right, preferred_element_type=f32)


def dot_g(left, right):
    return lax.dot_general(left, right, (((0,), (0,)), ((), ())), preferred_element_type=f32)


def attn_kernel(
    window, key_seg, seg, cosine, sine, pick, q_rows, kv_slots, o_slots, gains_r,
    query_o, qrot_o, key_o, keys_o, values_o, prob_o, mixed_o, attn_o, resid_o, normed_o, kv_rows_o,
):
    g_attn, g_post, g_query, g_key = gains_r[0:1], gains_r[1:2], gains_r[4:5, :HD], gains_r[5:6, :HD]
    span = window.shape[0]
    rows = seg.shape[0]
    halo = span - rows
    wf = window[...].astype(f32)
    normed_all = (wf * rms_rate(wf) * g_attn).astype(bf16)
    normed_o[...] = normed_all
    normed = normed_all[halo:]
    k_rows = dot_n(pick[...], kv_slots[:HD]).astype(bf16)
    v_rows = dot_n(pick[...], kv_slots[HD:]).astype(bf16)
    kv_rows_o[:HD] = k_rows
    kv_rows_o[HD:] = v_rows
    key = dot_t(normed_all, k_rows)
    key_o[...] = key
    values = dot_t(normed_all, v_rows).astype(bf16)
    values_o[...] = values
    keys = turn(key * rms_rate(key) * g_key, cosine[...], sine[...]).astype(bf16)
    keys_o[...] = keys
    cos_q, sin_q = cosine[halo:], sine[halo:]
    ahead = (
        lax.broadcasted_iota(jnp.int32, (rows, span), 0)
        + halo
        - lax.broadcasted_iota(jnp.int32, (rows, span), 1)
    )
    wide = (key_seg[...] == seg[...]) & (ahead >= 0) & (ahead < WINDOW)
    attn = jnp.zeros((rows, window.shape[1]), f32)
    for h in range(H):
        cols = slice(h * HD, (h + 1) * HD)
        query = dot_t(normed, q_rows[cols, :])
        query_o[:, cols] = query
        qrot = (turn(query * rms_rate(query) * g_query, cos_q, sin_q) * SCALE).astype(bf16)
        qrot_o[:, cols] = qrot
        scores = dot_t(qrot, keys)
        weight = jnp.where(wide, jnp.exp(scores), 0.0)
        prob = weight * (1.0 / jnp.sum(weight, axis=-1, keepdims=True))
        prob_o[h] = prob
        mixed = dot_n(prob.astype(bf16), values).astype(bf16)
        mixed_o[:, cols] = mixed
        attn = attn + dot_n(mixed, o_slots[cols, :])
    attn_o[...] = attn
    resid_o[...] = wf[halo:] + attn * rms_rate(attn) * g_post


C1, C2 = 0.7978845608028654, 0.044715


def rows_of(piece, i):
    part = piece[:, i]
    return part.reshape(part.shape[0] * part.shape[1], part.shape[2])


def ff_half(pieces, grads, kept, ffw_in, d_ffw_b, d_ffwin):
    for p in (3, 1, 2, 0):
        gate, up, hidden = kept(p)
        w_gate, w_up, w_down = (rows_of(pieces[p], i) for i in range(3))
        d_hidden = dot_t(d_ffw_b, w_down)
        t = jnp.tanh(C1 * (gate + C2 * (gate * gate * gate)))
        slope = 0.5 * (1.0 + t) + 0.5 * gate * (1.0 - t * t) * (C1 * (1.0 + 3.0 * C2 * gate * gate))
        d_gate = (d_hidden * up * slope).astype(bf16)
        d_up = (d_hidden * (0.5 * gate * (1.0 + t))).astype(bf16)
        for i, (left, right) in enumerate(((d_gate, ffw_in), (d_up, ffw_in), (hidden, d_ffw_b))):
            out = grads[p]
            out[:, i] = dot_g(left, right).astype(bf16).reshape(out.shape[0], out.shape[2], out.shape[3])
        d_ffwin = d_ffwin + dot_n(d_gate, w_gate) + dot_n(d_up, w_up)
    return d_ffwin


def ff_kernel(*refs):
    resid_r, cot_r, gains_r = refs[:3]
    g_ffw, g_final = gains_r[2:3], gains_r[3:4]
    pieces = refs[3:11]
    output_o, ffw_in_o, d_ffw_o, d_ffwin_o, gains_o = refs[11:16]
    grads = refs[16:20]
    gate_o, up_o, hidden_o, gate_s, up_s, hidden_s = refs[20:]
    resid = resid_r[...]
    cot = cot_r[...].astype(f32)
    ffw_in = (resid * rms_rate(resid) * g_ffw).astype(bf16)
    ffw_in_o[...] = ffw_in
    ffw_out = jnp.zeros(resid.shape, f32)
    for p in range(8):
        gate_d, up_d, hidden_d = ((gate_s, up_s, hidden_s), (gate_o, up_o, hidden_o))[p // 4]
        gate = dot_t(ffw_in, rows_of(pieces[p], 0))
        up = dot_t(ffw_in, rows_of(pieces[p], 1))
        t = jnp.tanh(C1 * (gate + C2 * (gate * gate * gate)))
        hidden = (0.5 * gate * (1.0 + t) * up).astype(bf16)
        gate_d[p % 4] = gate
        up_d[p % 4] = up
        hidden_d[p % 4] = hidden
        ffw_out = ffw_out + dot_n(hidden, rows_of(pieces[p], 2))
    out_rate = rms_rate(ffw_out)
    output_o[...] = (resid + ffw_out * out_rate * g_final).astype(bf16)
    d_ffw, gr_final = norm_grad(ffw_out, out_rate, g_final, cot)
    d_ffw_b = d_ffw.astype(bf16)
    d_ffw_o[...] = d_ffw_b
    gains_o[...] = gr_final
    d_ffwin_o[...] = ff_half(
        pieces[:4],
        grads,
        lambda p: (gate_s[p], up_s[p], hidden_s[p]),
        ffw_in,
        d_ffw_b,
        jnp.zeros(resid.shape, f32),
    )


def ff_rest_kernel(*refs):
    resid_r, attn_r, cot_r, gains_r, ffw_in_r, d_ffw_r, d_ffwin_r, gate_r, up_r, hidden_r = refs[:10]
    g_post, g_ffw = gains_r[1:2], gains_r[2:3]
    pieces = refs[10:14]
    d_resid_o, d_attn_o, gains_o = refs[14:17]
    grads = refs[17:]
    d_ffwin = ff_half(
        pieces,
        grads,
        lambda p: (gate_r[p], up_r[p], hidden_r[p]),
        ffw_in_r[...],
        d_ffw_r[...],
        d_ffwin_r[...],
    )
    resid = resid_r[...]
    d_res, gr_ffw = norm_grad(resid, rms_rate(resid), g_ffw, d_ffwin)
    d_resid = cot_r[...].astype(f32) + d_res
    d_resid_o[...] = d_resid
    attn = attn_r[...]
    d_attn, gr_post = norm_grad(attn, rms_rate(attn), g_post, d_resid)
    d_attn_o[...] = d_attn.astype(bf16)
    gains_o[0:1] = gr_post
    gains_o[1:2] = gr_ffw


def back_kernel(
    d_attn_r, window, normed_r, cosine, sine, pick, q_rows, kv_rows, o_slots, gains_r,
    query_r, qrot_r, key_r, keys_r, values_r, prob_r, mixed_r,
    q_grad_o, kv_grad_o, o_grad_o, d_halo_o, d_own_o, gr_attn_o, gr_head_o,
):
    g_query, g_key = gains_r[4:5, :HD], gains_r[5:6, :HD]
    span, width = window.shape
    rows = d_attn_r.shape[0]
    halo = span - rows
    d_attn = d_attn_r[...]
    normed_all = normed_r[...]
    normed = normed_all[halo:]
    keys, values = keys_r[...], values_r[...]
    cos_q, sin_q = cosine[halo:], sine[halo:]
    d_keys = jnp.zeros((span, HD), f32)
    d_values = jnp.zeros((span, HD), f32)
    d_own = jnp.zeros((rows, width), f32)
    gr_query = jnp.zeros((1, HD), f32)
    for h in range(H):
        cols = slice(h * HD, (h + 1) * HD)
        mixed = mixed_r[:, cols]
        o_grad_o[cols, :] = dot_g(mixed, d_attn).astype(bf16)
        d_mixed = dot_t(d_attn, o_slots[cols, :]).astype(bf16)
        prob = prob_r[h]
        d_probs = dot_t(d_mixed, values)
        delta = jnp.sum(d_mixed.astype(f32) * mixed.astype(f32), axis=-1, keepdims=True)
        d_scores = (prob * (d_probs - delta)).astype(bf16)
        d_qrot = dot_n(d_scores, keys) * SCALE
        d_keys = d_keys + dot_g(d_scores, qrot_r[:, cols])
        d_values = d_values + dot_g(prob.astype(bf16), d_mixed)
        query = query_r[:, cols]
        d_query, gr = norm_grad(query, rms_rate(query), g_query, turn_back(d_qrot, cos_q, sin_q))
        gr_query = gr_query + gr
        d_query_b = d_query.astype(bf16)
        q_grad_o[cols, :] = dot_g(d_query_b, normed).astype(bf16)
        d_own = d_own + dot_n(d_query_b, q_rows[cols, :])
    key = key_r[...]
    d_key, gr_key = norm_grad(key, rms_rate(key), g_key, turn_back(d_keys, cosine[...], sine[...]))
    d_key_b = d_key.astype(bf16)
    d_val_b = d_values.astype(bf16)
    kv_grad_o[:HD] = dot_g(dot_n(d_key_b, pick[...]).astype(bf16), normed_all).astype(bf16)
    kv_grad_o[HD:] = dot_g(dot_n(d_val_b, pick[...]).astype(bf16), normed_all).astype(bf16)
    d_window = dot_n(d_key_b, kv_rows[:HD]) + dot_n(d_val_b, kv_rows[HD:])
    d_halo_o[...] = d_window[:halo].astype(bf16)
    d_own = d_own + d_window[halo:]
    d_own_o[...] = d_own
    wf = window[...].astype(f32)
    scaled = wf * rms_rate(wf)
    gr_attn_o[...] = jnp.sum(scaled[:halo] * d_window[:halo], axis=0, keepdims=True) + jnp.sum(
        scaled[halo:] * d_own, axis=0, keepdims=True
    )
    gr_head_o[0:1] = gr_query
    gr_head_o[1:2] = gr_key


def call(kernel, outs, args, flops, scratch=()):
    nbytes = sum(a.size * a.dtype.itemsize for a in args) + sum(o.size * o.dtype.itemsize for o in outs)
    return pl.pallas_call(
        kernel,
        out_shape=outs,
        in_specs=[pl.BlockSpec(memory_space=pltpu.VMEM)] * len(args),
        out_specs=[pl.BlockSpec(memory_space=pltpu.VMEM)] * len(outs),
        scratch_shapes=list(scratch),
        cost_estimate=pl.CostEstimate(flops=flops, bytes_accessed=nbytes, transcendentals=0),
        compiler_params=pltpu.CompilerParams(vmem_limit_bytes=56 * 1024 * 1024),
    )(*args)


def like(shape, dtype):
    return jax.ShapeDtypeStruct(shape, dtype)


def body(
    hidden_in,
    segment_ids,
    cotangent,
    query_weight,
    key_weight,
    value_weight,
    out_weight,
    gate_weight,
    up_weight,
    down_weight,
    gain_attn,
    gain_query,
    gain_key,
    gain_post,
    gain_ffw,
    gain_final,
):
    peers = lax.axis_size("dp")
    me = lax.axis_index("dp")
    middle, quad = plan(peers)
    forth, back = middle, middle[::-1]
    count = len(middle)
    rows, width = hidden_in.shape
    reach = (WINDOW + rows - 1) // rows
    halo = reach * rows
    span = halo + rows
    q_block = query_weight.shape[1]
    k_block = key_weight.shape[1]
    f_block = gate_weight.shape[1]
    f_half = f_block // 2
    heads = q_block * peers
    twos = (2,) * count
    inner = (2,) * (count - 1)

    qt, kt, vt, gt, ut = (w.T for w in (query_weight, key_weight, value_weight, gate_weight, up_weight))
    attn_shard = jnp.concatenate([qt, kt, vt, out_weight], axis=0)
    attn_quad = jnp.stack(quad_swaps(attn_shard, quad))
    qkv = q_block + 2 * k_block

    ids = jnp.zeros((8, width), bf16).at[0, :rows].set(segment_ids.astype(bf16))
    mine = jnp.concatenate([hidden_in, ids], axis=0)
    before = [shifted(mine, hop) for hop in range(reach, 0, -1)]

    ff_shard = jnp.stack([w.reshape(2, f_half, width) for w in (gt, ut, down_weight)], axis=1)
    ff_shards = quad_swaps(ff_shard, quad)
    qkv_wide = widen(attn_quad[:, :qkv], forth)
    o_wide = widen(attn_quad[:, qkv:], back)
    small = (segment_ids, gain_attn, gain_query, gain_key, gain_post, gain_ffw, gain_final, me)
    (segment_ids, gain_attn, gain_query, gain_key, gain_post, gain_ffw, gain_final, me), qkv_wide, o_wide = (
        lax.optimization_barrier((small, qkv_wide, o_wide))
    )
    qkv_pieces = finish(qkv_wide, forth)
    o_pieces = finish(o_wide, back)
    ff_shards = after(ff_shards, (qkv_wide, o_wide))
    ff_quad = jnp.stack(ff_shards, axis=2)
    ff_quads = lax.optimization_barrier([ff_quad[0], ff_quad[1]])
    wide_a = widen(ff_quads[0], forth)
    wide_b = widen(ff_quads[1], back)
    before, qkv_pieces, o_pieces = after((before, qkv_pieces, o_pieces), (wide_a, wide_b))
    ff_a = finish(wide_a, forth)
    ff_b = finish(wide_b, back)

    tail = (count + 2, count + 3)
    to_slots = (count + 1,) + tuple(range(1, count + 1)) + (0,) + tail
    to_slots_b = (count + 1,) + tuple(range(count, 0, -1)) + (0,) + tail

    def slots(pieces, order):
        whole = jnp.stack(pieces).reshape((2, 2) + pieces[0].shape)
        return whole.transpose(order)

    qkv_slots = slots(qkv_pieces, to_slots).reshape(peers, qkv, width)
    o_slots = slots(o_pieces, to_slots_b).reshape(heads, width)
    q_rows = qkv_slots[:, :q_block].reshape(heads, width)
    kv_slots = jnp.concatenate(
        [qkv_slots[:, q_block : q_block + k_block].reshape(HD, width), qkv_slots[:, q_block + k_block :].reshape(HD, width)]
    )

    per_head = peers // H
    bits = me & (per_head - 1)
    place = jnp.arange(HD, dtype=jnp.int32)
    feature = ((place // q_block) ^ bits) * q_block + place % q_block
    source = (me ^ (feature // k_block)) * k_block + feature % k_block
    pick = lax.optimization_barrier((source[:, None] == place[None, :]).astype(bf16))
    gq = xor_blocks(gain_query, per_head, bits)
    gk = xor_blocks(gain_key, per_head, bits)
    spare = jnp.zeros((width - HD,), f32)
    gains_in = jnp.concatenate(
        [gain_attn, gain_post, gain_ffw, gain_final, gq, spare, gk, spare, jnp.zeros((2 * width,), f32)]
    ).reshape(8, width)
    half = HD // 2
    freq = jnp.power(BASE, -((feature[:half] % half).astype(f32) * (2.0 / HD)))
    theta = jnp.arange(span, dtype=jnp.int32).astype(f32)[:, None] * freq[None, :]
    cosine = jnp.cos(theta)
    sine = jnp.sin(theta) * jnp.where(feature[0] >= half, -1.0, 1.0)

    window = jnp.concatenate([b[:rows] for b in before] + [hidden_in], axis=0)
    seg = segment_ids.astype(f32)
    key_seg = jnp.concatenate([b[rows, :rows].astype(f32) for b in before] + [seg])
    key_idx = me * rows - halo + jnp.arange(span, dtype=jnp.int32)
    key_seg = jnp.where(key_idx >= 0, key_seg, -1.0)[None]

    query, qrot, key, keys, values, prob, mixed, attn, resid, normed_all, kv_rows = call(
        attn_kernel,
        [
            like((rows, heads), f32),
            like((rows, heads), bf16),
            like((span, HD), f32),
            like((span, HD), bf16),
            like((span, HD), bf16),
            like((H, rows, span), f32),
            like((rows, heads), bf16),
            like((rows, width), f32),
            like((rows, width), f32),
            like((span, width), bf16),
            like((2 * HD, width), bf16),
        ],
        (window, key_seg, seg[:, None], cosine, sine, pick, q_rows, kv_slots, o_slots, gains_in),
        flops=4_000_000_000,
    )

    def flat(piece):
        return piece.reshape(-1, 3, 4 * f_half, width)

    ff_a, ff_b = ([flat(p) for p in pieces] for pieces in (ff_a, ff_b))
    unit = ff_a[0].size // (3 * width)
    grads = [like(ff_a[0].shape, bf16)] * 4
    kept = [((4, rows, unit), f32), ((4, rows, unit), f32), ((4, rows, unit), bf16)]
    output, ffw_in, d_ffw, d_ffwin, gr_final, *rest = call(
        ff_kernel,
        [
            like((rows, width), bf16),
            like((rows, width), bf16),
            like((rows, width), bf16),
            like((rows, width), f32),
            like((1, width), f32),
        ]
        + grads
        + [like(*k) for k in kept],
        (resid, cotangent, gains_in, *ff_a, *ff_b),
        flops=4_000_000_000,
        scratch=[pltpu.VMEM(*k) for k in kept],
    )
    grads_a, kept_b = rest[:4], rest[4:]
    d_resid, d_attn, gr_two, *grads_b = call(
        ff_rest_kernel,
        [like((rows, width), f32), like((rows, width), bf16), like((2, width), f32)] + grads,
        (resid, attn, cotangent, gains_in, ffw_in, d_ffw, d_ffwin, *kept_b, *ff_b),
        flops=2_000_000_000,
    )

    q_grad, kv_grad, o_grad, d_halo, d_own, gr_attn, gr_head = call(
        back_kernel,
        [
            like((heads, width), bf16),
            like((2 * HD, width), bf16),
            like((heads, width), bf16),
            like((halo, width), bf16),
            like((rows, width), f32),
            like((1, width), f32),
            like((2, HD), f32),
        ],
        (d_attn, window, normed_all, cosine, sine, pick, q_rows, kv_rows, o_slots, gains_in)
        + (query, qrot, key, keys, values, prob, mixed),
        flops=6_000_000_000,
    )

    quads = []
    for parts, order in ((grads_a, forth), (grads_b, back)):
        far = added(parts[1], swap(parts[3], 1))
        terms = [parts[0], swap(parts[2], 1), swap(far, order[-1])]
        terms = [t.reshape(inner + (3, 4, f_half, width)) for t in terms]
        for mask in order[:-1][::-1]:
            got = swap(added(*[t[1] for t in terms]), mask)
            terms = [t[0] for t in terms] + [got]
        quads.append(terms)
    ff_ready = [[added(*[t[:, k] for t in terms]) for terms in quads] for k in range(4)]
    ff_ready = [jnp.stack(r) for r in ff_ready]
    ff_sum = quad_sum(ff_ready, quad)

    gr_query = xor_blocks(gr_head[0], per_head, bits)
    gr_key = xor_blocks(gr_head[1], per_head, bits)
    gains = jnp.concatenate([gr_two[0], gr_two[1], gr_final[0], gr_attn[0], gr_query, gr_key])
    lanes = gains.shape[0]
    tall = -(-lanes // (8 * width)) * 8
    gains = jnp.pad(gains, (0, tall * width - lanes)).reshape(tall, width).astype(bf16)

    from_slots = (count + 1,) + tuple(range(1, count + 1)) + (0,) + tail
    from_slots_b = (count + 1,) + tuple(range(count, 0, -1)) + (0,) + tail
    lead = (4,) + twos + (2,)
    kv4 = kv_grad.reshape(2, peers, k_block, width)
    qkv_parts = jnp.concatenate([q_grad.reshape(peers, q_block, width), kv4[0], kv4[1]], axis=1)
    qkv_parts = qkv_parts.reshape(lead + (qkv, width)).transpose(from_slots)
    o_parts = o_grad.reshape(lead + (q_block, width)).transpose(from_slots_b)

    def ride(part, mask):
        packed = jnp.concatenate([part.reshape(-1, width), gains], axis=0)
        got = swap(packed, mask)
        return got[:-tall].reshape(part.shape), plus(gains, got[-tall:])

    o_parts = plus(o_parts[0], swap(o_parts[1], 1))
    got, gains = ride(qkv_parts[1], 1)
    qkv_parts = plus(qkv_parts[0], got)
    for j in range(count):
        packed = jnp.concatenate([qkv_parts[1].reshape(-1, width), gains], axis=0)
        got = [swap(packed, back[j]), swap(o_parts[1], forth[j])]
        if j == 0:
            got = after(got, ff_ready[1:])
        gains = plus(gains, got[0][-tall:])
        qkv_parts = plus(qkv_parts[0], got[0][:-tall].reshape(qkv_parts.shape[1:]))
        o_parts = plus(o_parts[0], got[1])
    last = [jnp.concatenate([qkv_parts[k], o_parts[k], gains], axis=0) for k in range(4)]
    last = lax.optimization_barrier(last)
    attn_sum = quad_sum(last, quad)
    gains = attn_sum[qkv + q_block :].reshape(-1)
    sums = []
    at = 0
    for size in (width, width, width, width, HD, HD):
        sums.append(gains[at : at + size])
        at = at + size
    sum_post, sum_ffw, sum_final, sum_attn, sum_query, sum_key = sums

    returned = [shifted(d_halo[(reach - hop) * rows : (reach - hop + 1) * rows], -hop) for hop in range(1, reach + 1)]
    returned = after(returned, last)
    for part in returned:
        d_own = d_own + part.astype(f32)
    xf = hidden_in.astype(f32)
    scaled = d_own * gains_in[0:1]
    rate = lax.optimization_barrier(rms_rate(xf))
    unit_rows = lax.optimization_barrier(xf * (rate * rate))
    d_in = rate * (scaled - unit_rows * jnp.mean(scaled * xf, axis=-1, keepdims=True))
    input_grad = (d_resid + d_in).astype(bf16)

    def joined(i):
        return ff_sum[:, i].reshape(f_block, width)

    return (
        output,
        input_grad,
        attn_sum[:q_block].T,
        attn_sum[q_block : q_block + k_block].T,
        attn_sum[q_block + k_block : qkv].T,
        attn_sum[qkv : qkv + q_block],
        joined(0).T,
        joined(1).T,
        joined(2),
        sum_attn,
        sum_query,
        sum_key,
        sum_post,
        sum_ffw,
        sum_final,
    )


def solution(mesh):
    rows = P("dp", None)
    columns = P(None, "dp")
    in_specs = (rows, P("dp"), rows, columns, columns, columns, rows, columns, columns, rows) + (P(),) * 6
    out_specs = (rows, rows, columns, columns, columns, rows, columns, columns, rows) + (P(),) * 6

    return jax.shard_map(body, mesh=mesh, in_specs=in_specs, out_specs=out_specs, check_vma=False)
```

```python
import jax
import jax.numpy as jnp
from jax import lax
from jax.experimental import pallas as pl
from jax.experimental.pallas import tpu as pltpu
from jax.sharding import PartitionSpec as P


H = 4
HD = 256
WINDOW = 512

EPS = 1e-06
SCALE = 0.0625
BASE = 10000.0


f32 = jnp.float32
bf16 = jnp.bfloat16


def swap(array, mask):
    peers = lax.axis_size("dp")
    return lax.ppermute(array, "dp", [(i, i ^ mask) for i in range(peers)])


def shifted(array, by):
    peers = lax.axis_size("dp")
    pairs = [(i, i + by) for i in range(peers) if 0 <= i + by < peers]
    return lax.ppermute(array, "dp", pairs)


def plan(peers):
    quad = peers // 4
    middle = []
    mask = 2
    while mask < quad:
        middle.append(mask)
        mask = mask * 2
    return middle, quad


def widen(shard, order):
    for mask in order[:-1]:
        shard = lax.optimization_barrier(jnp.stack([shard, swap(shard, mask)]))
    return shard


def finish(shard, order):
    other = swap(shard, order[-1])
    return [shard, other, swap(shard, 1), swap(other, 1)]


def quad_swaps(shard, quad):
    return [shard] + [swap(shard, k * quad) for k in (1, 2, 3)]


def plus(left, right):
    return (left.astype(f32) + right.astype(f32)).astype(bf16)


def quad_sum(parts, quad):
    got = [swap(parts[k], k * quad).astype(f32) for k in (1, 2, 3)]
    return (parts[0].astype(f32) + got[0]) + (got[1] + got[2])


def after(array, first):
    return lax.optimization_barrier((array, first))[0]


def added(*terms):
    total = terms[0].astype(f32)
    for term in terms[1:]:
        total = total + term.astype(f32)
    return total.astype(bf16)


def rms_rate(value):
    return lax.rsqrt(jnp.mean(value * value, axis=-1, keepdims=True) + EPS)


def norm_grad(value, rate, gain, incoming):
    scaled = incoming * gain
    inner = jnp.mean(scaled * value, axis=-1, keepdims=True)
    dv = rate * (scaled - value * (rate * rate * inner))
    return dv, jnp.sum(incoming * value * rate, axis=0, keepdims=True)


def turn(value, cosine, sine):
    half = value.shape[-1] // 2
    first, second = value[:, :half], value[:, half:]
    return jnp.concatenate([first * cosine - second * sine, second * cosine + first * sine], axis=-1)


def turn_back(value, cosine, sine):
    half = value.shape[-1] // 2
    first, second = value[:, :half], value[:, half:]
    return jnp.concatenate([first * cosine + second * sine, second * cosine - first * sine], axis=-1)


def xor_blocks(vector, blocks, bits):
    rows = vector.reshape(blocks, -1)
    mask = 1
    while mask < blocks:
        pairs = rows.reshape(blocks // (2 * mask), 2, mask, -1)
        rows = jnp.where((bits & mask) != 0, pairs[:, ::-1], pairs).reshape(blocks, -1)
        mask = mask * 2
    return rows.reshape(vector.shape)


def dot_t(left, right):
    return lax.dot_general(left, right, (((1,), (1,)), ((), ())), preferred_element_type=f32)


def dot_n(left, right):
    return jnp.dot(left, right, preferred_element_type=f32)


def dot_g(left, right):
    return lax.dot_general(left, right, (((0,), (0,)), ((), ())), preferred_element_type=f32)


def attn_kernel(*refs):
    (
        mine, seg, cosine, sine, pick, q_rows, kv_slots, o_slots, gains_r,
        query_o, qrot_o, key_o, keys_o, values_o, prob_o, mixed_o, attn_o, resid_o, normed_o, kv_rows_o, window,
    ) = refs[-21:]
    parts = refs[:-21] + (mine,)
    g_attn, g_post, g_query, g_key = gains_r[0:1], gains_r[1:2], gains_r[4:5, :HD], gains_r[5:6, :HD]
    span = window.shape[0]
    rows = seg.shape[0]
    for i, part in enumerate(parts):
        window[i * rows : (i + 1) * rows, :] = part[:rows, :]
    key_seg = jnp.concatenate([part[rows : rows + 8, :rows].astype(f32)[0:1] for part in parts], axis=1)
    halo = span - rows
    wf = window[...].astype(f32)
    normed_all = (wf * rms_rate(wf) * g_attn).astype(bf16)
    normed_o[...] = normed_all
    normed = normed_all[halo:]
    k_rows = dot_n(pick[...], kv_slots[:HD]).astype(bf16)
    v_rows = dot_n(pick[...], kv_slots[HD:]).astype(bf16)
    kv_rows_o[:HD] = k_rows
    kv_rows_o[HD:] = v_rows
    key = dot_t(normed_all, k_rows)
    key_o[...] = key
    values = dot_t(normed_all, v_rows).astype(bf16)
    values_o[...] = values
    keys = turn(key * rms_rate(key) * g_key, cosine[...], sine[...]).astype(bf16)
    keys_o[...] = keys
    cos_q, sin_q = cosine[halo:], sine[halo:]
    ahead = (
        lax.broadcasted_iota(jnp.int32, (rows, span), 0)
        + halo
        - lax.broadcasted_iota(jnp.int32, (rows, span), 1)
    )
    wide = (key_seg == seg[...]) & (ahead >= 0) & (ahead < WINDOW)
    attn = jnp.zeros((rows, window.shape[1]), f32)
    for h in range(H):
        cols = slice(h * HD, (h + 1) * HD)
        query = dot_t(normed, q_rows[cols, :])
        query_o[:, cols] = query
        qrot = (turn(query * rms_rate(query) * g_query, cos_q, sin_q) * SCALE).astype(bf16)
        qrot_o[:, cols] = qrot
        scores = dot_t(qrot, keys)
        weight = jnp.where(wide, jnp.exp(scores), 0.0)
        prob = weight * (1.0 / jnp.sum(weight, axis=-1, keepdims=True))
        prob_o[h] = prob
        mixed = dot_n(prob.astype(bf16), values).astype(bf16)
        mixed_o[:, cols] = mixed
        attn = attn + dot_n(mixed, o_slots[cols, :])
    attn_o[...] = attn
    resid_o[...] = wf[halo:] + attn * rms_rate(attn) * g_post


C1, C2 = 0.7978845608028654, 0.044715


def rows_of(piece, i):
    part = piece[:, i]
    return part.reshape(part.shape[0] * part.shape[1], part.shape[2])


def ff_half(pieces, grads, kept, ffw_in, d_ffw_b, d_ffwin):
    for p in (3, 1, 2, 0):
        gate, up, hidden = kept(p)
        w_gate, w_up, w_down = (rows_of(pieces[p], i) for i in range(3))
        d_hidden = dot_t(d_ffw_b, w_down)
        t = jnp.tanh(C1 * (gate + C2 * (gate * gate * gate)))
        slope = 0.5 * (1.0 + t) + 0.5 * gate * (1.0 - t * t) * (C1 * (1.0 + 3.0 * C2 * gate * gate))
        d_gate = (d_hidden * up * slope).astype(bf16)
        d_up = (d_hidden * (0.5 * gate * (1.0 + t))).astype(bf16)
        for i, (left, right) in enumerate(((d_gate, ffw_in), (d_up, ffw_in), (hidden, d_ffw_b))):
            out = grads[p]
            out[:, i] = dot_g(left, right).astype(bf16).reshape(out.shape[0], out.shape[2], out.shape[3])
        d_ffwin = d_ffwin + dot_n(d_gate, w_gate) + dot_n(d_up, w_up)
    return d_ffwin


def ff_kernel(*refs):
    resid_r, cot_r, gains_r = refs[:3]
    g_ffw, g_final = gains_r[2:3], gains_r[3:4]
    pieces = refs[3:11]
    output_o, ffw_in_o, d_ffw_o, d_ffwin_o, gains_o = refs[11:16]
    grads = refs[16:20]
    gate_o, up_o, hidden_o, gate_s, up_s, hidden_s = refs[20:]
    resid = resid_r[...]
    cot = cot_r[...].astype(f32)
    ffw_in = (resid * rms_rate(resid) * g_ffw).astype(bf16)
    ffw_in_o[...] = ffw_in
    ffw_out = jnp.zeros(resid.shape, f32)
    for p in range(8):
        gate_d, up_d, hidden_d = ((gate_s, up_s, hidden_s), (gate_o, up_o, hidden_o))[p // 4]
        gate = dot_t(ffw_in, rows_of(pieces[p], 0))
        up = dot_t(ffw_in, rows_of(pieces[p], 1))
        t = jnp.tanh(C1 * (gate + C2 * (gate * gate * gate)))
        hidden = (0.5 * gate * (1.0 + t) * up).astype(bf16)
        gate_d[p % 4] = gate
        up_d[p % 4] = up
        hidden_d[p % 4] = hidden
        ffw_out = ffw_out + dot_n(hidden, rows_of(pieces[p], 2))
    out_rate = rms_rate(ffw_out)
    output_o[...] = (resid + ffw_out * out_rate * g_final).astype(bf16)
    d_ffw, gr_final = norm_grad(ffw_out, out_rate, g_final, cot)
    d_ffw_b = d_ffw.astype(bf16)
    d_ffw_o[...] = d_ffw_b
    gains_o[...] = gr_final
    d_ffwin_o[...] = ff_half(
        pieces[:4],
        grads,
        lambda p: (gate_s[p], up_s[p], hidden_s[p]),
        ffw_in,
        d_ffw_b,
        jnp.zeros(resid.shape, f32),
    )


def ff_rest_kernel(*refs):
    resid_r, attn_r, cot_r, gains_r, ffw_in_r, d_ffw_r, d_ffwin_r, gate_r, up_r, hidden_r = refs[:10]
    g_post, g_ffw = gains_r[1:2], gains_r[2:3]
    pieces = refs[10:14]
    d_resid_o, d_attn_o, gains_o = refs[14:17]
    grads = refs[17:]
    d_ffwin = ff_half(
        pieces,
        grads,
        lambda p: (gate_r[p], up_r[p], hidden_r[p]),
        ffw_in_r[...],
        d_ffw_r[...],
        d_ffwin_r[...],
    )
    resid = resid_r[...]
    d_res, gr_ffw = norm_grad(resid, rms_rate(resid), g_ffw, d_ffwin)
    d_resid = cot_r[...].astype(f32) + d_res
    d_resid_o[...] = d_resid
    attn = attn_r[...]
    d_attn, gr_post = norm_grad(attn, rms_rate(attn), g_post, d_resid)
    d_attn_o[...] = d_attn.astype(bf16)
    gains_o[0:1] = gr_post
    gains_o[1:2] = gr_ffw


def back_kernel(
    d_attn_r, window, normed_r, cosine, sine, pick, q_rows, kv_rows, o_slots, gains_r,
    query_r, qrot_r, key_r, keys_r, values_r, prob_r, mixed_r,
    q_grad_o, kv_grad_o, o_grad_o, d_halo_o, d_own_o, gr_attn_o, gr_head_o,
):
    g_query, g_key = gains_r[4:5, :HD], gains_r[5:6, :HD]
    span, width = window.shape
    rows = d_attn_r.shape[0]
    halo = span - rows
    d_attn = d_attn_r[...]
    normed_all = normed_r[...]
    normed = normed_all[halo:]
    keys, values = keys_r[...], values_r[...]
    cos_q, sin_q = cosine[halo:], sine[halo:]
    d_keys = jnp.zeros((span, HD), f32)
    d_values = jnp.zeros((span, HD), f32)
    d_own = jnp.zeros((rows, width), f32)
    gr_query = jnp.zeros((1, HD), f32)
    for h in range(H):
        cols = slice(h * HD, (h + 1) * HD)
        mixed = mixed_r[:, cols]
        o_grad_o[cols, :] = dot_g(mixed, d_attn).astype(bf16)
        d_mixed = dot_t(d_attn, o_slots[cols, :]).astype(bf16)
        prob = prob_r[h]
        d_probs = dot_t(d_mixed, values)
        delta = jnp.sum(d_mixed.astype(f32) * mixed.astype(f32), axis=-1, keepdims=True)
        d_scores = (prob * (d_probs - delta)).astype(bf16)
        d_qrot = dot_n(d_scores, keys) * SCALE
        d_keys = d_keys + dot_g(d_scores, qrot_r[:, cols])
        d_values = d_values + dot_g(prob.astype(bf16), d_mixed)
        query = query_r[:, cols]
        d_query, gr = norm_grad(query, rms_rate(query), g_query, turn_back(d_qrot, cos_q, sin_q))
        gr_query = gr_query + gr
        d_query_b = d_query.astype(bf16)
        q_grad_o[cols, :] = dot_g(d_query_b, normed).astype(bf16)
        d_own = d_own + dot_n(d_query_b, q_rows[cols, :])
    key = key_r[...]
    d_key, gr_key = norm_grad(key, rms_rate(key), g_key, turn_back(d_keys, cosine[...], sine[...]))
    d_key_b = d_key.astype(bf16)
    d_val_b = d_values.astype(bf16)
    kv_grad_o[:HD] = dot_g(dot_n(d_key_b, pick[...]).astype(bf16), normed_all).astype(bf16)
    kv_grad_o[HD:] = dot_g(dot_n(d_val_b, pick[...]).astype(bf16), normed_all).astype(bf16)
    d_window = dot_n(d_key_b, kv_rows[:HD]) + dot_n(d_val_b, kv_rows[HD:])
    d_halo_o[...] = d_window[:halo].astype(bf16)
    d_own = d_own + d_window[halo:]
    d_own_o[...] = d_own
    wf = window[...].astype(f32)
    scaled = wf * rms_rate(wf)
    gr_attn_o[...] = jnp.sum(scaled[:halo] * d_window[:halo], axis=0, keepdims=True) + jnp.sum(
        scaled[halo:] * d_own, axis=0, keepdims=True
    )
    gr_head_o[0:1] = gr_query
    gr_head_o[1:2] = gr_key


def call(kernel, outs, args, flops, scratch=()):
    nbytes = sum(a.size * a.dtype.itemsize for a in args) + sum(o.size * o.dtype.itemsize for o in outs)
    return pl.pallas_call(
        kernel,
        out_shape=outs,
        in_specs=[pl.BlockSpec(memory_space=pltpu.VMEM)] * len(args),
        out_specs=[pl.BlockSpec(memory_space=pltpu.VMEM)] * len(outs),
        scratch_shapes=list(scratch),
        cost_estimate=pl.CostEstimate(flops=flops, bytes_accessed=nbytes, transcendentals=0),
        compiler_params=pltpu.CompilerParams(vmem_limit_bytes=56 * 1024 * 1024),
    )(*args)


def like(shape, dtype):
    return jax.ShapeDtypeStruct(shape, dtype)


def body(
    hidden_in,
    segment_ids,
    cotangent,
    query_weight,
    key_weight,
    value_weight,
    out_weight,
    gate_weight,
    up_weight,
    down_weight,
    gain_attn,
    gain_query,
    gain_key,
    gain_post,
    gain_ffw,
    gain_final,
):
    peers = lax.axis_size("dp")
    me = lax.axis_index("dp")
    middle, quad = plan(peers)
    forth, back = middle, middle[::-1]
    count = len(middle)
    rows, width = hidden_in.shape
    reach = (WINDOW + rows - 1) // rows
    halo = reach * rows
    span = halo + rows
    q_block = query_weight.shape[1]
    k_block = key_weight.shape[1]
    f_block = gate_weight.shape[1]
    f_half = f_block // 2
    heads = q_block * peers
    twos = (2,) * count
    inner = (2,) * (count - 1)

    qt, kt, vt, gt, ut = (w.T for w in (query_weight, key_weight, value_weight, gate_weight, up_weight))
    attn_shard = jnp.concatenate([qt, kt, vt, out_weight], axis=0)
    attn_quad = jnp.stack(quad_swaps(attn_shard, quad))
    qkv = q_block + 2 * k_block

    ids = jnp.zeros((8, width), bf16).at[0, :rows].set((segment_ids + 1).astype(bf16))
    mine = jnp.concatenate([hidden_in, ids], axis=0)
    even = (me & 1) == 0
    hops = [mine] + [shifted(mine, hop) for hop in range(2, reach + 1, 2)]

    ff_shard = jnp.stack([w.reshape(2, f_half, width) for w in (gt, ut, down_weight)], axis=1)
    ff_shards = quad_swaps(ff_shard, quad)
    qkv_wide = widen(attn_quad[:, :qkv], forth)
    o_wide = widen(attn_quad[:, qkv:], back)
    small = (segment_ids, gain_attn, gain_query, gain_key, gain_post, gain_ffw, gain_final, me)
    (segment_ids, gain_attn, gain_query, gain_key, gain_post, gain_ffw, gain_final, me), qkv_wide, o_wide = (
        lax.optimization_barrier((small, qkv_wide, o_wide))
    )
    qkv_pieces = finish(qkv_wide, forth)
    o_pieces = finish(o_wide, back)
    ff_shards = after(ff_shards, (qkv_wide, o_wide))
    ff_quad = jnp.stack(ff_shards, axis=2)
    ff_quads = lax.optimization_barrier([ff_quad[0], ff_quad[1]])
    wide_a = widen(ff_quads[0], forth)
    wide_b = widen(ff_quads[1], back)
    hops, qkv_pieces, o_pieces = after((hops, qkv_pieces, o_pieces), (wide_a, wide_b))
    theirs = swap(jnp.stack(hops), 1)
    before = []
    for k in range(reach // 2, 0, -1):
        before += [hops[k], jnp.where(even, theirs[k], theirs[k - 1])]
    ff_a = finish(wide_a, forth)
    ff_b = finish(wide_b, back)

    tail = (count + 2, count + 3)
    to_slots = (count + 1,) + tuple(range(1, count + 1)) + (0,) + tail
    to_slots_b = (count + 1,) + tuple(range(count, 0, -1)) + (0,) + tail

    def slots(pieces, order):
        whole = jnp.stack(pieces).reshape((2, 2) + pieces[0].shape)
        return whole.transpose(order)

    qkv_slots = slots(qkv_pieces, to_slots).reshape(peers, qkv, width)
    o_slots = slots(o_pieces, to_slots_b).reshape(heads, width)
    q_rows = qkv_slots[:, :q_block].reshape(heads, width)
    kv_slots = jnp.concatenate(
        [qkv_slots[:, q_block : q_block + k_block].reshape(HD, width), qkv_slots[:, q_block + k_block :].reshape(HD, width)]
    )

    per_head = peers // H
    bits = me & (per_head - 1)
    place = jnp.arange(HD, dtype=jnp.int32)
    feature = ((place // q_block) ^ bits) * q_block + place % q_block
    source = (me ^ (feature // k_block)) * k_block + feature % k_block
    pick = lax.optimization_barrier((source[:, None] == place[None, :]).astype(bf16))
    gq = xor_blocks(gain_query, per_head, bits)
    gk = xor_blocks(gain_key, per_head, bits)
    spare = jnp.zeros((width - HD,), f32)
    gains_in = jnp.concatenate(
        [gain_attn, gain_post, gain_ffw, gain_final, gq, spare, gk, spare, jnp.zeros((2 * width,), f32)]
    ).reshape(8, width)
    half = HD // 2
    freq = jnp.power(BASE, -((feature[:half] % half).astype(f32) * (2.0 / HD)))
    theta = jnp.arange(span, dtype=jnp.int32).astype(f32)[:, None] * freq[None, :]
    cosine = jnp.cos(theta)
    sine = jnp.sin(theta) * jnp.where(feature[0] >= half, -1.0, 1.0)

    seg = (segment_ids + 1).astype(f32)

    query, qrot, key, keys, values, prob, mixed, attn, resid, normed_all, kv_rows, window = call(
        attn_kernel,
        [
            like((rows, heads), f32),
            like((rows, heads), bf16),
            like((span, HD), f32),
            like((span, HD), bf16),
            like((span, HD), bf16),
            like((H, rows, span), f32),
            like((rows, heads), bf16),
            like((rows, width), f32),
            like((rows, width), f32),
            like((span, width), bf16),
            like((2 * HD, width), bf16),
            like((span, width), bf16),
        ],
        (*before, mine, seg[:, None], cosine, sine, pick, q_rows, kv_slots, o_slots, gains_in),
        flops=4_000_000_000,
    )

    def flat(piece):
        return piece.reshape(-1, 3, 4 * f_half, width)

    ff_a, ff_b = ([flat(p) for p in pieces] for pieces in (ff_a, ff_b))
    unit = ff_a[0].size // (3 * width)
    grads = [like(ff_a[0].shape, bf16)] * 4
    kept = [((4, rows, unit), f32), ((4, rows, unit), f32), ((4, rows, unit), bf16)]
    output, ffw_in, d_ffw, d_ffwin, gr_final, *rest = call(
        ff_kernel,
        [
            like((rows, width), bf16),
            like((rows, width), bf16),
            like((rows, width), bf16),
            like((rows, width), f32),
            like((1, width), f32),
        ]
        + grads
        + [like(*k) for k in kept],
        (resid, cotangent, gains_in, *ff_a, *ff_b),
        flops=4_000_000_000,
        scratch=[pltpu.VMEM(*k) for k in kept],
    )
    grads_a, kept_b = rest[:4], rest[4:]
    d_resid, d_attn, gr_two, *grads_b = call(
        ff_rest_kernel,
        [like((rows, width), f32), like((rows, width), bf16), like((2, width), f32)] + grads,
        (resid, attn, cotangent, gains_in, ffw_in, d_ffw, d_ffwin, *kept_b, *ff_b),
        flops=2_000_000_000,
    )

    q_grad, kv_grad, o_grad, d_halo, d_own, gr_attn, gr_head = call(
        back_kernel,
        [
            like((heads, width), bf16),
            like((2 * HD, width), bf16),
            like((heads, width), bf16),
            like((halo, width), bf16),
            like((rows, width), f32),
            like((1, width), f32),
            like((2, HD), f32),
        ],
        (d_attn, window, normed_all, cosine, sine, pick, q_rows, kv_rows, o_slots, gains_in)
        + (query, qrot, key, keys, values, prob, mixed),
        flops=6_000_000_000,
    )

    quads = []
    for parts, order in ((grads_a, forth), (grads_b, back)):
        far = added(parts[1], swap(parts[3], 1))
        terms = [parts[0], swap(parts[2], 1), swap(far, order[-1])]
        terms = [t.reshape(inner + (3, 4, f_half, width)) for t in terms]
        for mask in order[:-1][::-1]:
            got = swap(added(*[t[1] for t in terms]), mask)
            terms = [t[0] for t in terms] + [got]
        quads.append(terms)
    ff_ready = [[added(*[t[:, k] for t in terms]) for terms in quads] for k in range(4)]
    ff_ready = [jnp.stack(r) for r in ff_ready]
    ff_sum = quad_sum(ff_ready, quad)

    gr_query = xor_blocks(gr_head[0], per_head, bits)
    gr_key = xor_blocks(gr_head[1], per_head, bits)
    gains = jnp.concatenate([gr_two[0], gr_two[1], gr_final[0], gr_attn[0], gr_query, gr_key])
    lanes = gains.shape[0]
    tall = -(-lanes // (8 * width)) * 8
    gains = jnp.pad(gains, (0, tall * width - lanes)).reshape(tall, width).astype(bf16)

    from_slots = (count + 1,) + tuple(range(1, count + 1)) + (0,) + tail
    from_slots_b = (count + 1,) + tuple(range(count, 0, -1)) + (0,) + tail
    lead = (4,) + twos + (2,)
    kv4 = kv_grad.reshape(2, peers, k_block, width)
    qkv_parts = jnp.concatenate([q_grad.reshape(peers, q_block, width), kv4[0], kv4[1]], axis=1)
    qkv_parts = qkv_parts.reshape(lead + (qkv, width)).transpose(from_slots)
    o_parts = o_grad.reshape(lead + (q_block, width)).transpose(from_slots_b)

    def ride(part, mask):
        packed = jnp.concatenate([part.reshape(-1, width), gains], axis=0)
        got = swap(packed, mask)
        return got[:-tall].reshape(part.shape), plus(gains, got[-tall:])

    o_parts = plus(o_parts[0], swap(o_parts[1], 1))
    got, gains = ride(qkv_parts[1], 1)
    qkv_parts = plus(qkv_parts[0], got)
    for j in range(count):
        packed = jnp.concatenate([qkv_parts[1].reshape(-1, width), gains], axis=0)
        got = [swap(packed, back[j]), swap(o_parts[1], forth[j])]
        if j == 0:
            got = after(got, ff_ready[1:])
        gains = plus(gains, got[0][-tall:])
        qkv_parts = plus(qkv_parts[0], got[0][:-tall].reshape(qkv_parts.shape[1:]))
        o_parts = plus(o_parts[0], got[1])
    last = [jnp.concatenate([qkv_parts[k], o_parts[k], gains], axis=0) for k in range(4)]
    last = lax.optimization_barrier(last)
    attn_sum = quad_sum(last, quad)
    gains = attn_sum[qkv + q_block :].reshape(-1)
    sums = []
    at = 0
    for size in (width, width, width, width, HD, HD):
        sums.append(gains[at : at + size])
        at = at + size
    sum_post, sum_ffw, sum_final, sum_attn, sum_query, sum_key = sums

    away = [d_halo[(reach - hop) * rows : (reach - hop + 1) * rows] for hop in range(1, reach + 1)]
    theirs = swap(jnp.stack(away[::2]), 1)
    zero = jnp.zeros_like(theirs[0])
    own = jnp.where(even, theirs[0], zero)
    returned = []
    for k in range(1, reach // 2 + 1):
        later = theirs[k] if k < reach // 2 else zero
        packed = plus(away[2 * k - 1], jnp.where(even, later, theirs[k - 1]))
        returned.append(shifted(packed, -2 * k))
    own, returned = after((own, returned), last)
    for part in [own] + returned:
        d_own = d_own + part.astype(f32)
    xf = hidden_in.astype(f32)
    scaled = d_own * gains_in[0:1]
    rate = lax.optimization_barrier(rms_rate(xf))
    unit_rows = xf * (rate * rate)
    d_in = rate * (scaled - unit_rows * jnp.mean(scaled * xf, axis=-1, keepdims=True))
    input_grad = (d_resid + d_in).astype(bf16)

    def joined(i):
        return ff_sum[:, i].reshape(f_block, width)

    return (
        output,
        input_grad,
        attn_sum[:q_block].T,
        attn_sum[q_block : q_block + k_block].T,
        attn_sum[q_block + k_block : qkv].T,
        attn_sum[qkv : qkv + q_block],
        joined(0).T,
        joined(1).T,
        joined(2),
        sum_attn,
        sum_query,
        sum_key,
        sum_post,
        sum_ffw,
        sum_final,
    )


def solution(mesh):
    rows = P("dp", None)
    columns = P(None, "dp")
    in_specs = (rows, P("dp"), rows, columns, columns, columns, rows, columns, columns, rows) + (P(),) * 6
    out_specs = (rows, rows, columns, columns, columns, rows, columns, columns, rows) + (P(),) * 6

    return jax.shard_map(body, mesh=mesh, in_specs=in_specs, out_specs=out_specs, check_vma=False)
```
